1024 devices in a mesh: ctx: 8 (over y, core), tp: 16 (over x, z_hi), section: 8 (over z_lo).
Axes of the slice: x: 4, y: 4, z: 32 (z_hi: 4, z_lo: 8; z = z_hi * 8 + z_lo), core: 2. Of those that a mesh axis runs over, the one named last changes fastest.
Arguments:
- queries: bfloat16 [2, 8192, 8192], P(None, ('ctx', 'section'), 'tp'), may hold values from -15 to 15
- self_kv: bfloat16 [2, 8192, 2048], P(None, ('ctx', 'section')), may hold values from -6 to 6
- image_kv: bfloat16 [1024, 2048], P(('ctx', 'tp', 'section')), may hold values from -6 to 6
- cross_gate: float32 [64], P('tp'), may hold values from 0.3 to 2
- lengths: int32 [2], replicated, may hold values from 2048 to 8192, as said below
Outputs:
- attended: bfloat16 [2, 8192, 8192], P(None, ('ctx', 'section'), 'tp')
The draws below stay inside these ranges and needn't reach their ends.
Inputs may be any that keep to these rules, and one draw needn't show every extreme that they name: `lengths`: one of the two sequences uses all 8192 positions, the other fewer.
All inputs are finite; a program needn't handle non-finite values.
Results may differ from the reference program's by a relative error of at most 0.004.
Values may be sent and summed in bfloat16 or wider, within the bound.
A program may use at most 128 MiB of HBM per device.

```python
import math
import jax
import jax.numpy as jnp
from jax import lax

HQ = 64
KVH = 8
HEAD_SIZE = 128
SEQ_LEN = 8192
IMG_TOKENS = 1024


def unit_noise(key, shape):
    return jnp.clip(jax.random.normal(key, shape, jnp.float32), -6.0, 6.0)


def draw_queries(key, part):
    base = 2.5 * unit_noise(jax.random.fold_in(key, 1), (2, SEQ_LEN, HQ, HEAD_SIZE))
    return base.reshape(2, SEQ_LEN, HQ * HEAD_SIZE).astype(jnp.bfloat16)


def draw_self_kv(key, part):
    base = unit_noise(jax.random.fold_in(key, 4), (2, SEQ_LEN, KVH, 2, HEAD_SIZE))
    return base.reshape(2, SEQ_LEN, KVH * 2 * HEAD_SIZE).astype(jnp.bfloat16)


def draw_image_kv(key, part):
    base = unit_noise(jax.random.fold_in(key, 5), (IMG_TOKENS, KVH, 2, HEAD_SIZE))
    return base.reshape(IMG_TOKENS, KVH * 2 * HEAD_SIZE).astype(jnp.bfloat16)


def draw_lengths(key, part):
    full_index = jax.random.randint(jax.random.fold_in(key, 21), (), 0, 2)
    shorter = jax.random.randint(jax.random.fold_in(key, 22), (), SEQ_LEN // 4, SEQ_LEN)
    slots = jnp.arange(2, dtype=jnp.int32)
    return jnp.where(slots == full_index, SEQ_LEN, shorter).astype(jnp.int32)


def block_levels(rng, extent, pieces, smallest, largest):
    def one(dim, blocks):
        heights = jax.random.uniform(jax.random.fold_in(jax.random.fold_in(rng, 6), dim), (blocks,), jnp.float32, smallest / len(pieces), largest / len(pieces))
        return jnp.repeat(jnp.exp(heights), extent[dim] // blocks).reshape((-1,) + (1,) * (len(extent) - dim - 1))

    loudness = one(*pieces[0])
    for cut in pieces[1:]:
        loudness = loudness * one(*cut)
    return loudness


def setup_inputs(seed: int = 0) -> dict:
    seeds = jax.random.split(jax.random.key(seed), 6)
    queries = draw_queries(jax.random.fold_in(seeds[5], 71), 0)
    self_kv = draw_self_kv(jax.random.fold_in(seeds[5], 71), 0)
    image_kv = draw_image_kv(jax.random.fold_in(seeds[5], 71), 0)
    cross_gate = jnp.clip(0.3 + 1.7 * jax.random.uniform(seeds[3], (HQ,), jnp.float32) ** block_levels(seeds[3], (HQ,), ((0, 16),), -0.2, 0.2), 0.3, 2.0)
    lengths = draw_lengths(jax.random.fold_in(seeds[5], 71), 0)
    return dict(queries=queries, self_kv=self_kv, image_kv=image_kv, cross_gate=cross_gate, lengths=lengths)


neg_large = -1e+30

def attend(query_matrix, key_matrix, value_matrix, allowed):
    logit_scores = jnp.einsum('hnz,hfz->hnf', query_matrix.astype(jnp.float32), key_matrix.astype(jnp.float32)) * (1.0 / math.sqrt(HEAD_SIZE))
    masked = jnp.where(allowed, logit_scores, neg_large)
    row_best = lax.optimization_barrier(jnp.max(masked, axis=-1, keepdims=True))
    weights = jnp.where(allowed, jnp.exp(masked - row_best), 0.0)
    row_total = lax.optimization_barrier(jnp.sum(weights, axis=-1, keepdims=True))
    rounded_scores = weights.astype(jnp.bfloat16)
    summed_output = jnp.einsum('eug,egr->eur', rounded_scores.astype(jnp.float32), value_matrix.astype(jnp.float32))
    return summed_output / row_total

def reference(queries, self_kv, image_kv, cross_gate, lengths):
    seq_len = queries.shape[1]
    image_rows = image_kv.shape[0]
    heads_per_group = HQ // KVH
    head_queries = jnp.transpose(queries.reshape(2, seq_len, HQ, HEAD_SIZE), (2, 0, 1, 3))
    kv_pairs = self_kv.reshape(2, seq_len, KVH, 2, HEAD_SIZE)
    self_keys = jnp.transpose(kv_pairs[:, :, :, 0], (2, 0, 1, 3))
    self_values = jnp.transpose(kv_pairs[:, :, :, 1], (2, 0, 1, 3))
    image_pairs = image_kv.reshape(image_rows, KVH, 2, HEAD_SIZE)
    image_keys = jnp.transpose(image_pairs[:, :, 0], (1, 0, 2))
    image_values = jnp.transpose(image_pairs[:, :, 1], (1, 0, 2))
    position = jnp.arange(seq_len, dtype=jnp.int32)
    allowed = (position[None, None, :] <= position[None, :, None]) & (position[None, None, :] < lengths.astype(jnp.int32)[:, None, None])
    everywhere = jnp.ones((1, 1, 1), jnp.bool_)

    def one_head(head_index):
        kv_index = head_index // heads_per_group
        query_one = lax.dynamic_index_in_dim(head_queries, head_index, 0, keepdims=False)
        key_one = lax.dynamic_index_in_dim(self_keys, kv_index, 0, keepdims=False)
        value_one = lax.dynamic_index_in_dim(self_values, kv_index, 0, keepdims=False)
        self_out = attend(query_one, key_one, value_one, allowed)
        image_key = jnp.broadcast_to(lax.dynamic_index_in_dim(image_keys, kv_index, 0, keepdims=True), (2, image_rows, HEAD_SIZE))
        image_value = jnp.broadcast_to(lax.dynamic_index_in_dim(image_values, kv_index, 0, keepdims=True), (2, image_rows, HEAD_SIZE))
        cross_out = attend(query_one, image_key, image_value, everywhere)
        gate_factor = jnp.tanh(lax.dynamic_index_in_dim(cross_gate, head_index, 0, keepdims=False))
        return (self_out + gate_factor * cross_out).astype(jnp.bfloat16)
    per_head = lax.map(one_head, jnp.arange(HQ, dtype=jnp.int32))
    return jnp.transpose(per_head, (1, 2, 0, 3)).reshape(2, seq_len, HQ * HEAD_SIZE)
```

```python
import functools
import math

import jax
import jax.numpy as jnp
from jax import lax
from jax.experimental import pallas as pl
from jax.experimental.pallas import tpu as pltpu
from jax.sharding import PartitionSpec as P

HQ = 64
KVH = 8
D = 128
B = 128
ZL = 8
ZR = 32
Y = 4
X = 4
ROWS = 512
CHUNK = 512
NEG = -1e30
SCALE = math.log2(math.e) / math.sqrt(D)
MESH = pl.DeviceIdType.MESH


def attention_kernel(
    q_ref, kv_ref, img_ref, gate_ref, len_ref, out_ref,
    kv_all, rows, img_all, qt, acc, best, total,
    kv_recv, z_send, up_send, down_send, mate_send,
    row_recv, row_right, row_left, x_recv, x_send, img_recv, img_send, local,
):
    ctx = lax.axis_index("ctx")
    tp = lax.axis_index("tp")
    z = lax.axis_index("section")
    y, c = ctx // 2, ctx % 2
    x, zh = tp // 4, tp % 4
    zp = zh * ZL + z
    head = tp // 2
    rank = ctx * ZL + z

    def z_ring(step):
        at = (zp + step + ZR) % ZR
        return {"tp": x * 4 + at // ZL, "section": at % ZL}

    right, left = z_ring(1), z_ring(-1)
    up = {"ctx": ((y + 1) % Y) * 2 + c}
    down = {"ctx": ((y + Y - 1) % Y) * 2 + c}
    mate = {"ctx": y * 2 + (1 - c)}

    def x_peer(step):
        return {"tp": ((x + step) % X) * 4 + zh}

    def span(block):
        return pl.ds(pl.multiple_of(block * B, B), B)

    def piece(block, s):
        return kv_all.at[s, span(block), :]

    def remote(src, dst, send_sem, recv_sem, to):
        return pltpu.make_async_remote_copy(
            src_ref=src, dst_ref=dst, send_sem=send_sem, recv_sem=recv_sem,
            device_id=to, device_id_type=MESH,
        )

    def move(block, s, send_sem, to):
        return remote(piece(block, s), piece(block, s), send_sem, kv_recv.at[block * 2 + s], to)

    own_cols = pl.ds(pl.multiple_of(head * 2 * D, 2 * D), 2 * D)
    own_kv = [
        pltpu.make_async_copy(kv_ref.at[s, :, own_cols], piece(rank, s), local.at[s]) for s in (0, 1)
    ]
    own_row = pltpu.make_async_copy(img_ref, rows.at[zp], local.at[2])
    for cp in own_kv:
        cp.start()
    own_row.start()

    barrier = pltpu.get_barrier_semaphore()
    peers = (right, left, up, down, mate, x_peer(1), x_peer(2), x_peer(3))
    for peer in peers:
        pl.semaphore_signal(barrier, inc=1, device_id=peer, device_id_type=MESH)
    pl.semaphore_wait(barrier, len(peers))

    def row_move(at, send_sem, to):
        return remote(rows.at[at], rows.at[at], send_sem, row_recv.at[at], to)

    def row_step(j):
        from_left = (zp - 1 - j + 2 * ZR) % ZR
        from_right = (zp + 1 + j) % ZR
        row_move(from_left, row_right.at[0], right).wait_recv()

        @pl.when(j < 15)
        def _():
            row_move(from_left, row_right.at[j + 1], right).start()
            row_move(from_right, row_left.at[0], left).wait_recv()

        @pl.when(j < 14)
        def _():
            row_move(from_right, row_left.at[j + 1], left).start()

    def mate_slot(row, at, s):
        return mate_send.at[(row * ZL + at) * 2 + s]

    def block_of(row, at):
        return (row * 2 + c) * ZL + at

    def spread(at, s):
        block = block_of(y, at)
        move(block, s, up_send.at[at * 2 + s], up).start()
        move(block, s, down_send.at[at * 2 + s], down).start()
        move(block, s, mate_slot(y, at, s), mate).start()

    def z_step(d, s):
        @pl.when(z - d >= 0)
        def _():
            at = z - d
            move(block_of(y, at), s, z_send.at[at * 2 + s], right).wait_recv()

            @pl.when(z < ZL - 1)
            def _():
                move(block_of(y, at), s, z_send.at[at * 2 + s], right).start()

            spread(at, s)

        @pl.when(z + d < ZL)
        def _():
            at = z + d
            move(block_of(y, at), s, z_send.at[at * 2 + s], left).wait_recv()

            @pl.when(z > 0)
            def _():
                move(block_of(y, at), s, z_send.at[at * 2 + s], left).start()

            spread(at, s)

    below, above, across = (y + Y - 1) % Y, (y + 1) % Y, (y + 2) % Y

    def y_item(at, s):
        block = block_of(below, at)
        move(block, s, up_send.at[0], up).wait_recv()
        if s == 0:
            move(block, s, up_send.at[2 * ZL + at], up).start()
        move(block, s, mate_slot(below, at, s), mate).start()
        block = block_of(above, at)
        move(block, s, down_send.at[0], down).wait_recv()
        if s == 1:
            move(block, s, down_send.at[2 * ZL + at], down).start()
        move(block, s, mate_slot(above, at, s), mate).start()

    def across_item(at, s):
        block = block_of(across, at)
        move(block, s, up_send.at[0], up).wait_recv()
        move(block, s, mate_slot(across, at, s), mate).start()

    def both_sides(d, item):
        for s in (0, 1):
            @pl.when(z - d >= 0)
            def _():
                item(z - d, s)

            @pl.when(z + d < ZL)
            def _():
                item(z + d, s)

    own_row.wait()
    row_move(zp, row_right.at[0], right).start()
    row_move(zp, row_left.at[0], left).start()
    for s in (0, 1):
        own_kv[s].wait()

        @pl.when(z < ZL - 1)
        def _():
            move(rank, s, z_send.at[16 + s], right).start()

        @pl.when(z > 0)
        def _():
            move(rank, s, z_send.at[18 + s], left).start()

        spread(z, s)

    for s in (0, 1):
        for h in range(4):
            qt[s, :, h * B : (h + 1) * B] = q_ref[s, :, h * D : (h + 1) * D].T

    def gather_steps(d):
        for s in (0, 1):
            row_step(2 * (d - 1) + s)
            z_step(d, s)

    @pl.loop(0, 3)
    def _(t):
        gather_steps(2 * t + 1)
        gather_steps(2 * t + 2)

        @pl.when(t == 0)
        def _():
            y_item(z, 0)
            y_item(z, 1)

        @pl.when(t > 0)
        def _():
            both_sides(t, y_item)

    gather_steps(7)
    row_step(14)
    row_step(15)

    def head_rows(h):
        return rows.at[:, h]

    x_moves = []
    for step in (1, 2, 3):
        peer_head = 2 * ((x + step) % X) + zh // 2
        x_moves.append(
            remote(head_rows(peer_head), img_all.at[ctx, x], x_send.at[step], x_recv.at[x], x_peer(step))
        )
    own_head = pltpu.make_async_copy(head_rows(head), img_all.at[ctx, x], local.at[3])
    for cp in x_moves:
        cp.start()
    own_head.start()

    def img_move(at, send_sem, to):
        return remote(img_all.at[at], img_all.at[at], send_sem, img_recv.at[at], to)

    both_sides(3, y_item)
    own_head.wait()
    for step in (1, 2, 3):
        src = (x + X - step) % X
        remote(head_rows(head), img_all.at[ctx, src], x_send.at[0], x_recv.at[src], x_peer(1)).wait_recv()
    img_sends = [img_move(ctx, img_send.at[0], up), img_move(ctx, img_send.at[1], down), img_move(ctx, img_send.at[2], mate)]
    for cp in img_sends:
        cp.start()

    @pl.loop(4, ZL)
    def _(d):
        both_sides(d, y_item)

        @pl.when(d == 4)
        def _():
            across_item(z, 0)
            across_item(z, 1)

        @pl.when(d > 4)
        def _():
            both_sides(d - 4, across_item)

    at = below * 2 + c
    img_move(at, img_send.at[0], up).wait_recv()
    more = [img_move(at, img_send.at[3], up), img_move(at, img_send.at[4], mate)]
    for cp in more:
        cp.start()
    img_sends += more
    for slot, row in ((5, above), (6, across)):
        at = row * 2 + c
        img_move(at, img_send.at[0], up).wait_recv()
        cp = img_move(at, img_send.at[slot], mate)
        cp.start()
        img_sends.append(cp)

    @pl.loop(4, ZL)
    def _(d):
        both_sides(d, across_item)

    @pl.loop(0, Y)
    def _(row):
        img_move(row * 2 + 1 - c, img_send.at[0], mate).wait_recv()

        @pl.loop(0, ZL)
        def _(at):
            for s in (0, 1):
                move((row * 2 + 1 - c) * ZL + at, s, up_send.at[0], mate).wait_recv()

    key_iota = lax.broadcasted_iota(jnp.int32, (CHUNK, ROWS), 0)
    query_pos = rank * B + lax.broadcasted_iota(jnp.int32, (1, ROWS), 1) % B

    def start_rows():
        best[...] = jnp.full_like(best, NEG)
        total[...] = jnp.zeros_like(total)
        acc[...] = jnp.zeros_like(acc)

    def fold(s, keys, values, limit):
        scores = jnp.dot(keys, qt[s], preferred_element_type=jnp.float32) * SCALE
        if limit is not None:
            scores = jnp.where(key_iota < limit, scores, NEG)
        old = best[...]
        new = jnp.maximum(old, jnp.max(scores, axis=0, keepdims=True))
        weights = jnp.exp2(scores - new)
        shrink = jnp.exp2(old - new)
        best[...] = new
        total[...] = total[...] * shrink + jnp.sum(weights, axis=0, keepdims=True)
        acc[...] = acc[...] * shrink + lax.dot_general(
            values, weights.astype(jnp.bfloat16), (((0,), (0,)), ((), ())),
            preferred_element_type=jnp.float32,
        )

    gates = jnp.tanh(gate_ref[...])
    gate_row = jnp.concatenate(
        [jnp.broadcast_to(gates[:, h : h + 1], (1, B)) for h in range(4)], axis=1
    )
    for s in (0, 1):
        start_rows()
        limit = jnp.minimum(query_pos + 1, len_ref[s])

        @pl.loop(0, rank // (CHUNK // B) + 1)
        def _(n):
            first = pl.multiple_of(n * CHUNK, CHUNK)
            fold(
                s, kv_all[s, pl.ds(first, CHUNK), :D], kv_all[s, pl.ds(first, CHUNK), D:],
                limit - first,
            )

        self_out = acc[...] / total[...]
        start_rows()

        @pl.loop(0, 2)
        def _(n):
            pairs = img_all[pl.ds(4 * n, 4)]
            fold(s, pairs[:, :, :, 0].reshape(CHUNK, D), pairs[:, :, :, 1].reshape(CHUNK, D), None)

        attended = self_out + gate_row * (acc[...] / total[...])
        for h in range(4):
            out_ref[s, :, h * D : (h + 1) * D] = attended[:, h * B : (h + 1) * B].T.astype(jnp.bfloat16)

    for cp in x_moves + img_sends:
        cp.wait_send()

    @pl.loop(0, 16)
    def _(j):
        row_move(zp, row_right.at[j], right).wait_send()

    @pl.loop(0, 15)
    def _(j):
        row_move(zp, row_left.at[j], left).wait_send()

    for s in (0, 1):
        @pl.when(z < ZL - 1)
        def _():
            move(rank, s, z_send.at[16 + s], right).wait_send()

        @pl.when(z > 0)
        def _():
            move(rank, s, z_send.at[18 + s], left).wait_send()

    @pl.loop(0, ZL)
    def _(at):
        @pl.when(((at < z) & (z < ZL - 1)) | ((at > z) & (z > 0)))
        def _():
            for s in (0, 1):
                move(rank, s, z_send.at[at * 2 + s], right).wait_send()

    @pl.loop(0, 3 * ZL)
    def _(j):
        move(rank, 0, up_send.at[j], up).wait_send()
        move(rank, 0, down_send.at[j], down).wait_send()

    @pl.loop(0, 2 * Y * ZL)
    def _(j):
        move(rank, 0, mate_send.at[j], mate).wait_send()


def per_device(queries, self_kv, image_kv, cross_gate, lengths):
    vmem = pl.BlockSpec(memory_space=pltpu.VMEM)
    dma = pltpu.SemaphoreType.DMA
    return pl.pallas_call(
        attention_kernel,
        out_shape=jax.ShapeDtypeStruct(queries.shape, queries.dtype),
        in_specs=[
            vmem,
            pl.BlockSpec(memory_space=pl.ANY),
            vmem,
            vmem,
            pl.BlockSpec(memory_space=pltpu.SMEM),
        ],
        out_specs=vmem,
        scratch_shapes=[
            pltpu.VMEM((2, 64 * B, 2 * D), jnp.bfloat16),
            pltpu.VMEM((ZR, KVH, 2, D), jnp.bfloat16),
            pltpu.VMEM((8, X, ZR, 2, D), jnp.bfloat16),
            pltpu.VMEM((2, D, ROWS), jnp.bfloat16),
            pltpu.VMEM((D, ROWS), jnp.float32),
            pltpu.VMEM((1, ROWS), jnp.float32),
            pltpu.VMEM((1, ROWS), jnp.float32),
            dma((128,)),
            dma((20,)),
            dma((24,)),
            dma((24,)),
            dma((64,)),
            dma((ZR,)),
            dma((16,)),
            dma((15,)),
            dma((X,)),
            dma((X,)),
            dma((8,)),
            dma((7,)),
            dma((4,)),
        ],
        compiler_params=pltpu.CompilerParams(
            collective_id=0, has_side_effects=True, vmem_limit_bytes=56 * 1024 * 1024
        ),
    )(queries, self_kv, image_kv.reshape(KVH, 2, D), cross_gate.reshape(1, 4), lengths)


def solution(mesh):
    placed = (
        P(None, ("ctx", "section"), "tp"),
        P(None, ("ctx", "section"), None),
        P(("ctx", "tp", "section"), None),
        P("tp"),
        P(),
    )
    return jax.shard_map(
        per_device,
        mesh=mesh,
        in_specs=placed,
        out_specs=P(None, ("ctx", "section"), "tp"),
        check_vma=False,
    )
```

```python
import functools
import math

import jax
import jax.numpy as jnp
from jax import lax
from jax.experimental import pallas as pl
from jax.experimental.pallas import tpu as pltpu
from jax.sharding import PartitionSpec as P

HQ = 64
KVH = 8
D = 128
B = 128
ZL = 8
ZR = 32
Y = 4
X = 4
ROWS = 512
CHUNK = 512
EARLY = 20
MID = 2
NEG = -1e30
SCALE = math.log2(math.e) / math.sqrt(D)
MESH = pl.DeviceIdType.MESH


def attention_kernel(
    q_ref, kv_ref, img_ref, gate_ref, len_ref, out_ref,
    kv_all, xrows, img_all, qt, acc, best, total, self_out, limits,
    kv_recv, z_send, up_send, down_send, mate_send,
    x_recv, x_send, row_recv, row_send, img_recv, img_send, local, token,
):
    ctx = lax.axis_index("ctx")
    tp = lax.axis_index("tp")
    z = lax.axis_index("section")
    y, c = ctx // 2, ctx % 2
    x, zh = tp // 4, tp % 4
    zp = zh * ZL + z
    head = tp // 2
    rank = ctx * ZL + z

    def z_line(at):
        return {"tp": x * 4 + at // ZL, "section": at % ZL}

    right, left = z_line(jnp.minimum(zp + 1, ZR - 1)), z_line(jnp.maximum(zp - 1, 0))
    up = {"ctx": ((y + 1) % Y) * 2 + c}
    down = {"ctx": ((y + Y - 1) % Y) * 2 + c}
    mate = {"ctx": y * 2 + (1 - c)}

    def x_peer(step):
        return {"tp": ((x + step) % X) * 4 + zh}

    def span(block):
        return pl.ds(pl.multiple_of(block * B, B), B)

    def piece(block, s):
        return kv_all.at[s, span(block), :]

    def remote(src, dst, send_sem, recv_sem, to):
        return pltpu.make_async_remote_copy(
            src_ref=src, dst_ref=dst, send_sem=send_sem, recv_sem=recv_sem,
            device_id=to, device_id_type=MESH,
        )

    def move(block, s, send_sem, to):
        return remote(piece(block, s), piece(block, s), send_sem, kv_recv.at[block * 2 + s], to)

    own_cols = pl.ds(pl.multiple_of(head * 2 * D, 2 * D), 2 * D)
    own_kv = [
        pltpu.make_async_copy(kv_ref.at[s, :, own_cols], piece(rank, s), local.at[s]) for s in (0, 1)
    ]
    for cp in own_kv:
        cp.start()

    barrier = pltpu.get_barrier_semaphore()
    peers = (up, down, mate, x_peer(1), x_peer(2), x_peer(3))
    for peer in peers:
        pl.semaphore_signal(barrier, inc=1, device_id=peer, device_id_type=MESH)

    def greet(at):
        pl.semaphore_signal(barrier, inc=1, device_id=z_line(at), device_id_type=MESH)

    @pl.when(zp > 0)
    def _():
        greet(zp - 1)

    @pl.when((zp >= EARLY - 1) & (zp < ZR - 1))
    def _():
        greet(zp + 1)

    @pl.loop(zp + 1, EARLY)
    def _(at):
        greet(at)

    @pl.when(zp < ZL)
    def _():
        @pl.loop(EARLY, ZR)
        def _(at):
            greet(at)

    lower = jnp.where(zp < EARLY, zp, ZL)
    below_is_extra = jnp.where(zp < EARLY, 0, 1)
    above_is_there = jnp.where(zp < ZR - 1, 1, 0)
    pl.semaphore_wait(barrier, len(peers) + lower + below_is_extra + above_is_there)

    def x_move(to, src, step):
        return remote(img_ref.at[to], xrows.at[src], x_send.at[step], x_recv.at[src], x_peer(step))

    def row_move(to, src):
        return remote(
            xrows.at[:, to // 16], img_all.at[ctx, src], row_send.at[to], row_recv.at[src], z_line(to)
        )

    own_x = pltpu.make_async_copy(img_ref.at[x], xrows.at[x], local.at[2])
    own_z = pltpu.make_async_copy(xrows.at[:, zp // 16], img_all.at[ctx, zp], local.at[3])

    def rows_down():
        for step in (1, 2, 3):
            src = (x + X - step) % X
            x_move(x, src, step).wait_recv()
        own_x.wait()
        own_z.start()

        @pl.loop(0, lower)
        def _(at):
            row_move(at, zp).start()

        @pl.when(zp == EARLY - 1)
        def _():
            pl.semaphore_signal(token, inc=1, device_id=right, device_id_type=MESH)

    def rows_down_late():
        @pl.when(zp >= EARLY)
        def _():
            pl.semaphore_wait(token, 1)

            @pl.when(zp < ZR - 1)
            def _():
                pl.semaphore_signal(token, inc=1, device_id=right, device_id_type=MESH)

            @pl.loop(ZL, zp)
            def _(at):
                row_move(at, zp).start()

    def rows_back(first, last):
        @pl.loop(first, last)
        def _(at):
            row_move(at, at).wait_recv()
            row_move(at, zp).start()

    own_x.start()
    for step in (1, 2, 3):
        x_move((x + step) % X, x, step).start()

    def mate_slot(row, at, s):
        return mate_send.at[(row * ZL + at) * 2 + s]

    def block_of(row, at):
        return (row * 2 + c) * ZL + at

    def spread(at, s):
        block = block_of(y, at)
        move(block, s, up_send.at[at * 2 + s], up).start()
        move(block, s, down_send.at[at * 2 + s], down).start()
        move(block, s, mate_slot(y, at, s), mate).start()

    def z_step(d, s):
        @pl.when(z - d >= 0)
        def _():
            at = z - d
            move(block_of(y, at), s, z_send.at[at * 2 + s], right).wait_recv()

            @pl.when(z < ZL - 1)
            def _():
                move(block_of(y, at), s, z_send.at[at * 2 + s], right).start()

            spread(at, s)

        @pl.when(z + d < ZL)
        def _():
            at = z + d
            move(block_of(y, at), s, z_send.at[at * 2 + s], left).wait_recv()

            @pl.when(z > 0)
            def _():
                move(block_of(y, at), s, z_send.at[at * 2 + s], left).start()

            spread(at, s)

    below, above, across = (y + Y - 1) % Y, (y + 1) % Y, (y + 2) % Y

    def y_item(at, s):
        block = block_of(below, at)
        move(block, s, up_send.at[0], up).wait_recv()
        if s == 0:
            move(block, s, up_send.at[2 * ZL + at], up).start()
        move(block, s, mate_slot(below, at, s), mate).start()
        block = block_of(above, at)
        move(block, s, down_send.at[0], down).wait_recv()
        if s == 1:
            move(block, s, down_send.at[2 * ZL + at], down).start()
        move(block, s, mate_slot(above, at, s), mate).start()

    def across_item(at, s):
        block = block_of(across, at)
        move(block, s, up_send.at[0], up).wait_recv()
        move(block, s, mate_slot(across, at, s), mate).start()

    def both_sides(d, item):
        for s in (0, 1):
            @pl.when(z - d >= 0)
            def _():
                item(z - d, s)

            @pl.when(z + d < ZL)
            def _():
                item(z + d, s)

    for s in (0, 1):
        own_kv[s].wait()

        @pl.when(z < ZL - 1)
        def _():
            move(rank, s, z_send.at[16 + s], right).start()

        @pl.when(z > 0)
        def _():
            move(rank, s, z_send.at[18 + s], left).start()

        spread(z, s)

    for s in (0, 1):
        for h in range(4):
            qt[s, :, h * B : (h + 1) * B] = q_ref[s, :, h * D : (h + 1) * D].T

    key_iota = lax.broadcasted_iota(jnp.int32, (CHUNK, ROWS), 0)
    query_pos = rank * B + lax.broadcasted_iota(jnp.int32, (1, ROWS), 1) % B
    for s in (0, 1):
        limits[s] = jnp.minimum(query_pos + 1, len_ref[s])

    def start_rows():
        best[...] = jnp.full_like(best, NEG)
        total[...] = jnp.zeros_like(total)
        acc[...] = jnp.zeros_like(acc)

    def fold(s, keys, values, limit):
        scores = jnp.dot(keys, qt[s], preferred_element_type=jnp.float32) * SCALE
        if limit is not None:
            scores = jnp.where(key_iota < limit, scores, NEG)
        old = best[s]
        new = jnp.maximum(old, jnp.max(scores, axis=0, keepdims=True))
        weights = jnp.exp2(scores - new)
        shrink = jnp.exp2(old - new)
        best[s] = new
        total[s] = total[s] * shrink + jnp.sum(weights, axis=0, keepdims=True)
        acc[s] = acc[s] * shrink + lax.dot_general(
            values, weights.astype(jnp.bfloat16), (((0,), (0,)), ((), ())),
            preferred_element_type=jnp.float32,
        )

    near = z // 4
    far = 1 - near

    def fold_half(row, core, half):
        block = (row * 2 + core) * ZL + half * 4

        @pl.when(core != c)
        def _():
            @pl.loop(0, 4)
            def _(k):
                for s in (0, 1):
                    move(block + k, s, up_send.at[0], mate).wait_recv()

        @pl.when(block // 4 <= rank // 4)
        def _():
            first = pl.multiple_of(block * B, CHUNK)

            @pl.loop(0, 2)
            def _(s):
                fold(
                    s, kv_all[s, pl.ds(first, CHUNK), :D], kv_all[s, pl.ds(first, CHUNK), D:],
                    limits[s] - first,
                )

    def gather_steps(d):
        z_step(d, 0)
        z_step(d, 1)

    start_rows()
    rows_down()
    gather_steps(1)
    gather_steps(2)
    rows_down_late()
    y_item(z, 0)
    y_item(z, 1)
    gather_steps(3)

    @pl.loop(0, 2)
    def _(t):
        gather_steps(4 + 2 * t)
        fold_half(y, (c + t) % 2, near)
        both_sides(1 + t, y_item)
        gather_steps(5 + 2 * t)

    run_end = (zh + 1) * ZL
    rows_back(zp + 1, run_end)
    both_sides(3, y_item)

    def neighbour_row(t):
        return (y + 3 + 2 * (t // 2)) % Y

    @pl.loop(0, 2)
    def _(t):
        fold_half(y, (c + t) % 2, far)

    @pl.loop(0, MID)
    def _(t):
        both_sides(4 + t, y_item)

        @pl.when(t == 0)
        def _():
            across_item(z, 0)
            across_item(z, 1)

        @pl.when(t > 0)
        def _():
            both_sides(t, across_item)

        fold_half(neighbour_row(t), (c + t) % 2, near)

    rows_back(run_end, ZR)

    @pl.loop(MID, 4)
    def _(t):
        both_sides(4 + t, y_item)

        @pl.when(t == 0)
        def _():
            across_item(z, 0)
            across_item(z, 1)

        @pl.when(t > 0)
        def _():
            both_sides(t, across_item)

        fold_half(neighbour_row(t), (c + t) % 2, near)

    @pl.loop(0, zp)
    def _(at):
        row_move(zp, at).wait_recv()

    own_z.wait()

    def img_move(at, send_sem, to):
        return remote(img_all.at[at], img_all.at[at], send_sem, img_recv.at[at], to)

    img_sends = [img_move(ctx, img_send.at[0], up), img_move(ctx, img_send.at[1], down), img_move(ctx, img_send.at[2], mate)]
    for cp in img_sends:
        cp.start()

    @pl.loop(0, 4)
    def _(t):
        both_sides(4 + t, across_item)
        fold_half(neighbour_row(t), (c + t) % 2, far)

    at = below * 2 + c
    img_move(at, img_send.at[0], up).wait_recv()
    more = [img_move(at, img_send.at[3], up), img_move(at, img_send.at[4], mate)]
    for cp in more:
        cp.start()
    img_sends += more
    at = above * 2 + c
    img_move(at, img_send.at[0], up).wait_recv()
    cp = img_move(at, img_send.at[5], mate)
    cp.start()
    img_sends.append(cp)

    @pl.loop(0, 4)
    def _(t):
        fold_half(across, (c + t) % 2, (near + t // 2) % 2)

    at = across * 2 + c
    img_move(at, img_send.at[0], up).wait_recv()
    cp = img_move(at, img_send.at[6], mate)
    cp.start()
    img_sends.append(cp)

    for s in (0, 1):
        self_out[s] = acc[s] / total[s]
    start_rows()

    @pl.loop(0, Y)
    def _(row):
        img_move(row * 2 + 1 - c, img_send.at[0], mate).wait_recv()

    gates = jnp.tanh(gate_ref[...])
    gate_row = jnp.concatenate(
        [jnp.broadcast_to(gates[:, h : h + 1], (1, B)) for h in range(4)], axis=1
    )

    @pl.loop(0, 2)
    def _(n):
        pairs = img_all[pl.ds(4 * n, 4)]
        keys, values = pairs[:, :, :, 0].reshape(CHUNK, D), pairs[:, :, :, 1].reshape(CHUNK, D)
        for s in (0, 1):
            fold(s, keys, values, None)

    for s in (0, 1):
        attended = self_out[s] + gate_row * (acc[s] / total[s])
        for h in range(4):
            out_ref[s, :, h * D : (h + 1) * D] = attended[:, h * B : (h + 1) * B].T.astype(jnp.bfloat16)

    for cp in img_sends:
        cp.wait_send()
    for step in (1, 2, 3):
        x_move(x, x, step).wait_send()

    @pl.loop(0, ZR)
    def _(to):
        @pl.when(to != zp)
        def _():
            row_move(to, zp).wait_send()

    for s in (0, 1):
        @pl.when(z < ZL - 1)
        def _():
            move(rank, s, z_send.at[16 + s], right).wait_send()

        @pl.when(z > 0)
        def _():
            move(rank, s, z_send.at[18 + s], left).wait_send()

    @pl.loop(0, ZL)
    def _(at):
        @pl.when(((at < z) & (z < ZL - 1)) | ((at > z) & (z > 0)))
        def _():
            for s in (0, 1):
                move(rank, s, z_send.at[at * 2 + s], right).wait_send()

    @pl.loop(0, 3 * ZL)
    def _(j):
        move(rank, 0, up_send.at[j], up).wait_send()
        move(rank, 0, down_send.at[j], down).wait_send()

    @pl.loop(0, 2 * Y * ZL)
    def _(j):
        move(rank, 0, mate_send.at[j], mate).wait_send()


def per_device(queries, self_kv, image_kv, cross_gate, lengths):
    vmem = pl.BlockSpec(memory_space=pltpu.VMEM)
    dma = pltpu.SemaphoreType.DMA
    return pl.pallas_call(
        attention_kernel,
        out_shape=jax.ShapeDtypeStruct(queries.shape, queries.dtype),
        in_specs=[
            vmem,
            pl.BlockSpec(memory_space=pl.ANY),
            vmem,
            vmem,
            pl.BlockSpec(memory_space=pltpu.SMEM),
        ],
        out_specs=vmem,
        scratch_shapes=[
            pltpu.VMEM((2, 64 * B, 2 * D), jnp.bfloat16),
            pltpu.VMEM((X, 2, 2, D), jnp.bfloat16),
            pltpu.VMEM((8, ZR, X, 2, D), jnp.bfloat16),
            pltpu.VMEM((2, D, ROWS), jnp.bfloat16),
            pltpu.VMEM((2, D, ROWS), jnp.float32),
            pltpu.VMEM((2, 1, ROWS), jnp.float32),
            pltpu.VMEM((2, 1, ROWS), jnp.float32),
            pltpu.VMEM((2, D, ROWS), jnp.float32),
            pltpu.VMEM((2, 1, ROWS), jnp.int32),
            dma((128,)),
            dma((20,)),
            dma((24,)),
            dma((24,)),
            dma((64,)),
            dma((X,)),
            dma((X,)),
            dma((ZR,)),
            dma((ZR,)),
            dma((8,)),
            dma((7,)),
            dma((4,)),
            pltpu.SemaphoreType.REGULAR,
        ],
        compiler_params=pltpu.CompilerParams(
            collective_id=0, has_side_effects=True, vmem_limit_bytes=56 * 1024 * 1024
        ),
    )(queries, self_kv, image_kv.reshape(X, 2, 2, D), cross_gate.reshape(1, 4), lengths)


def solution(mesh):
    placed = (
        P(None, ("ctx", "section"), "tp"),
        P(None, ("ctx", "section"), None),
        P(("ctx", "tp", "section"), None),
        P("tp"),
        P(),
    )
    return jax.shard_map(
        per_device,
        mesh=mesh,
        in_specs=placed,
        out_specs=P(None, ("ctx", "section"), "tp"),
        check_vma=False,
    )
```

```python
import functools
import math

import jax
import jax.numpy as jnp
from jax import lax
from jax.experimental import pallas as pl
from jax.experimental.pallas import tpu as pltpu
from jax.sharding import PartitionSpec as P

HQ = 64
KVH = 8
D = 128
B = 128
ZL = 8
ZR = 32
Y = 4
X = 4
ROWS = 512
CHUNK = 512
EARLY = 20
NEG = -1e30
SCALE = math.log2(math.e) / math.sqrt(D)
MESH = pl.DeviceIdType.MESH


def attention_kernel(
    q_ref, kv_ref, img_ref, gate_ref, len_ref, out_ref,
    kv_all, xrows, img_all, qt, acc, best, total, limits,
    kv_recv, z_send, up_send, down_send, mate_send,
    x_recv, x_send, row_recv, row_send, img_recv, img_send, local, token,
):
    ctx = lax.axis_index("ctx")
    tp = lax.axis_index("tp")
    z = lax.axis_index("section")
    y, c = ctx // 2, ctx % 2
    x, zh = tp // 4, tp % 4
    zp = zh * ZL + z
    head = tp // 2
    rank = ctx * ZL + z

    def z_line(at):
        return {"tp": x * 4 + at // ZL, "section": at % ZL}

    right, left = z_line(jnp.minimum(zp + 1, ZR - 1)), z_line(jnp.maximum(zp - 1, 0))
    up = {"ctx": ((y + 1) % Y) * 2 + c}
    down = {"ctx": ((y + Y - 1) % Y) * 2 + c}
    mate = {"ctx": y * 2 + (1 - c)}

    def x_peer(step):
        return {"tp": ((x + step) % X) * 4 + zh}

    def span(block):
        return pl.ds(pl.multiple_of(block * B, B), B)

    def piece(block, s):
        return kv_all.at[s, span(block), :]

    def remote(src, dst, send_sem, recv_sem, to):
        return pltpu.make_async_remote_copy(
            src_ref=src, dst_ref=dst, send_sem=send_sem, recv_sem=recv_sem,
            device_id=to, device_id_type=MESH,
        )

    def move(block, s, send_sem, to):
        return remote(piece(block, s), piece(block, s), send_sem, kv_recv.at[block * 2 + s], to)

    own_cols = pl.ds(pl.multiple_of(head * 2 * D, 2 * D), 2 * D)
    own_kv = [
        pltpu.make_async_copy(kv_ref.at[s, :, own_cols], piece(rank, s), local.at[s]) for s in (0, 1)
    ]
    for cp in own_kv:
        cp.start()

    barrier = pltpu.get_barrier_semaphore()
    peers = (up, down, mate, x_peer(1), x_peer(2), x_peer(3))
    for peer in peers:
        pl.semaphore_signal(barrier, inc=1, device_id=peer, device_id_type=MESH)

    def greet(at):
        pl.semaphore_signal(barrier, inc=1, device_id=z_line(at), device_id_type=MESH)

    @pl.when(zp > 0)
    def _():
        greet(zp - 1)

    @pl.when((zp >= EARLY - 1) & (zp < ZR - 1))
    def _():
        greet(zp + 1)

    @pl.loop(zp + 1, EARLY)
    def _(at):
        greet(at)

    @pl.when(zp < ZL)
    def _():
        @pl.loop(EARLY, ZR)
        def _(at):
            greet(at)

    lower = jnp.where(zp < EARLY, zp, ZL)
    below_is_extra = jnp.where(zp < EARLY, 0, 1)
    above_is_there = jnp.where(zp < ZR - 1, 1, 0)
    pl.semaphore_wait(barrier, len(peers) + lower + below_is_extra + above_is_there)

    @pl.when(zp == EARLY - 1)
    def _():
        pl.semaphore_signal(token, inc=1, device_id=right, device_id_type=MESH)

    def x_move(to, src, step):
        return remote(img_ref.at[to], xrows.at[src], x_send.at[step], x_recv.at[src], x_peer(step))

    def row_move(to, src):
        return remote(
            xrows.at[:, to // 16], img_all.at[ctx, src], row_send.at[to], row_recv.at[src], z_line(to)
        )

    own_x = pltpu.make_async_copy(img_ref.at[x], xrows.at[x], local.at[2])
    own_z = pltpu.make_async_copy(xrows.at[:, zp // 16], img_all.at[ctx, zp], local.at[3])

    def rows_down():
        for step in (1, 2, 3):
            src = (x + X - step) % X
            x_move(x, src, step).wait_recv()
        own_x.wait()
        own_z.start()

        @pl.loop(0, lower)
        def _(at):
            row_move(at, zp).start()

    def rows_down_late():
        @pl.when(zp >= EARLY)
        def _():
            pl.semaphore_wait(token, 1)

            @pl.when(zp < ZR - 1)
            def _():
                pl.semaphore_signal(token, inc=1, device_id=right, device_id_type=MESH)

            @pl.loop(ZL, zp)
            def _(at):
                row_move(at, zp).start()

    def rows_back(first, last):
        @pl.loop(first, last)
        def _(at):
            row_move(at, at).wait_recv()
            row_move(at, zp).start()

    own_x.start()
    for step in (1, 2, 3):
        x_move((x + step) % X, x, step).start()

    def mate_slot(row, at, s):
        return mate_send.at[(row * ZL + at) * 2 + s]

    def block_of(row, at):
        return (row * 2 + c) * ZL + at

    def spread(at, s):
        block = block_of(y, at)
        move(block, s, up_send.at[at * 2 + s], up).start()
        move(block, s, down_send.at[at * 2 + s], down).start()
        move(block, s, mate_slot(y, at, s), mate).start()

    def z_step(d, s):
        @pl.when(z - d >= 0)
        def _():
            at = z - d
            move(block_of(y, at), s, z_send.at[at * 2 + s], right).wait_recv()

            @pl.when(z < ZL - 1)
            def _():
                move(block_of(y, at), s, z_send.at[at * 2 + s], right).start()

            spread(at, s)

        @pl.when(z + d < ZL)
        def _():
            at = z + d
            move(block_of(y, at), s, z_send.at[at * 2 + s], left).wait_recv()

            @pl.when(z > 0)
            def _():
                move(block_of(y, at), s, z_send.at[at * 2 + s], left).start()

            spread(at, s)

    below, above, across = (y + Y - 1) % Y, (y + 1) % Y, (y + 2) % Y

    def y_item(at, s):
        block = block_of(below, at)
        move(block, s, up_send.at[0], up).wait_recv()
        if s == 0:
            move(block, s, up_send.at[2 * ZL + at], up).start()
        move(block, s, mate_slot(below, at, s), mate).start()
        block = block_of(above, at)
        move(block, s, down_send.at[0], down).wait_recv()
        if s == 1:
            move(block, s, down_send.at[2 * ZL + at], down).start()
        move(block, s, mate_slot(above, at, s), mate).start()

    def across_item(at, s):
        block = block_of(across, at)
        move(block, s, up_send.at[0], up).wait_recv()
        move(block, s, mate_slot(across, at, s), mate).start()

    def both_sides(d, item):
        for s in (0, 1):
            @pl.when(z - d >= 0)
            def _():
                item(z - d, s)

            @pl.when(z + d < ZL)
            def _():
                item(z + d, s)

    for s in (0, 1):
        own_kv[s].wait()

        @pl.when(z < ZL - 1)
        def _():
            move(rank, s, z_send.at[16 + s], right).start()

        @pl.when(z > 0)
        def _():
            move(rank, s, z_send.at[18 + s], left).start()

        spread(z, s)

    for s in (0, 1):
        for h in range(4):
            qt[s, :, h * B : (h + 1) * B] = q_ref[s, :, h * D : (h + 1) * D].T

    key_iota = lax.broadcasted_iota(jnp.int32, (CHUNK, ROWS), 0)
    query_pos = rank * B + lax.broadcasted_iota(jnp.int32, (1, ROWS), 1) % B
    for s in (0, 1):
        limits[s] = jnp.minimum(query_pos + 1, len_ref[s])

    def start_rows():
        best[...] = jnp.full_like(best, NEG)
        total[...] = jnp.zeros_like(total)
        acc[...] = jnp.zeros_like(acc)

    def fold(jobs, at):
        scores = []
        for s, (keys, _, limit) in enumerate(jobs):
            raw = jnp.dot(keys, qt[s], preferred_element_type=jnp.float32) * SCALE
            scores.append(raw if limit is None else jnp.where(key_iota < limit, raw, NEG))
        for s, (_, values, _) in enumerate(jobs):
            old = best[at + s]
            new = jnp.maximum(old, jnp.max(scores[s], axis=0, keepdims=True))
            weights = jnp.exp2(scores[s] - new)
            shrink = jnp.exp2(old - new)
            best[at + s] = new
            total[at + s] = total[at + s] * shrink + jnp.sum(weights, axis=0, keepdims=True)
            acc[at + s] = acc[at + s] * shrink + lax.dot_general(
                values, weights.astype(jnp.bfloat16), (((0,), (0,)), ((), ())),
                preferred_element_type=jnp.float32,
            )

    near = z // 4
    far = 1 - near

    def fold_half(row, core, half):
        block = (row * 2 + core) * ZL + half * 4

        @pl.when(core != c)
        def _():
            @pl.loop(0, 4)
            def _(k):
                for s in (0, 1):
                    move(block + k, s, up_send.at[0], mate).wait_recv()

        @pl.when(block // 4 <= rank // 4)
        def _():
            first = pl.multiple_of(block * B, CHUNK)

            keys = pl.ds(first, CHUNK)
            fold([(kv_all[s, keys, :D], kv_all[s, keys, D:], limits[s] - first) for s in (0, 1)], 0)

    def gather_steps(d):
        z_step(d, 0)
        z_step(d, 1)

    start_rows()
    rows_down()
    gather_steps(1)
    rows_down_late()
    gather_steps(2)
    y_item(z, 0)
    y_item(z, 1)
    gather_steps(3)

    @pl.loop(0, 2)
    def _(t):
        gather_steps(4 + 2 * t)
        fold_half(y, (c + t) % 2, near)
        both_sides(1 + t, y_item)
        gather_steps(5 + 2 * t)

    run_end = (zh + 1) * ZL
    rows_back(zp + 1, run_end)
    both_sides(3, y_item)

    def neighbour_row(t):
        return (y + 3 + 2 * (t // 2)) % Y

    @pl.loop(0, 2)
    def _(t):
        fold_half(y, (c + t) % 2, far)

    @pl.when(zp >= ZL)
    def _():
        rows_back(run_end, ZR)

    @pl.loop(0, 4)
    def _(t):
        both_sides(4 + t, y_item)
        fold_half(neighbour_row(t), (c + t) % 2, near)

        @pl.when((t == 1) & (zp < ZL))
        def _():
            rows_back(run_end, ZR)

    across_item(z, 0)
    across_item(z, 1)

    @pl.loop(0, zp)
    def _(at):
        row_move(zp, at).wait_recv()

    own_z.wait()

    def img_move(at, send_sem, to):
        return remote(img_all.at[at], img_all.at[at], send_sem, img_recv.at[at], to)

    img_sends = [img_move(ctx, img_send.at[0], up), img_move(ctx, img_send.at[1], down), img_move(ctx, img_send.at[2], mate)]
    for cp in img_sends:
        cp.start()

    at_below, at_above, at_across = below * 2 + c, above * 2 + c, across * 2 + c
    img_relays = [
        img_move(at_below, img_send.at[3], up), img_move(at_below, img_send.at[4], mate),
        img_move(at_above, img_send.at[5], mate), img_move(at_across, img_send.at[6], mate),
    ]

    @pl.loop(0, 4)
    def _(t):
        fold_half(neighbour_row(t), (c + t) % 2, far)

        @pl.when(t < 3)
        def _():
            both_sides(1 + t, across_item)

    img_move(at_below, img_send.at[0], up).wait_recv()
    img_relays[0].start()
    img_relays[1].start()
    img_move(at_above, img_send.at[0], up).wait_recv()
    img_relays[2].start()

    @pl.loop(0, 2)
    def _(t):
        both_sides(4 + 2 * t, across_item)
        fold_half(across, (c + t) % 2, near)
        both_sides(5 + 2 * t, across_item)

    img_move(at_across, img_send.at[0], up).wait_recv()
    img_relays[3].start()

    @pl.loop(0, 2)
    def _(t):
        fold_half(across, (c + t) % 2, far)

    @pl.loop(0, Y)
    def _(row):
        img_move(row * 2 + 1 - c, img_send.at[0], mate).wait_recv()

    gates = jnp.tanh(gate_ref[...])
    gate_row = jnp.concatenate(
        [jnp.broadcast_to(gates[:, h : h + 1], (1, B)) for h in range(4)], axis=1
    )

    @pl.loop(0, 2)
    def _(n):
        pairs = img_all[pl.ds(4 * n, 4)]
        keys, values = pairs[:, :, :, 0].reshape(CHUNK, D), pairs[:, :, :, 1].reshape(CHUNK, D)
        fold([(keys, values, None)] * 2, 2)

    for s in (0, 1):
        attended = acc[s] / total[s] + gate_row * (acc[2 + s] / total[2 + s])
        for h in range(4):
            out_ref[s, :, h * D : (h + 1) * D] = attended[:, h * B : (h + 1) * B].T.astype(jnp.bfloat16)

    for cp in img_sends + img_relays:
        cp.wait_send()
    for step in (1, 2, 3):
        x_move(x, x, step).wait_send()

    @pl.loop(0, ZR)
    def _(to):
        @pl.when(to != zp)
        def _():
            row_move(to, zp).wait_send()

    for s in (0, 1):
        @pl.when(z < ZL - 1)
        def _():
            move(rank, s, z_send.at[16 + s], right).wait_send()

        @pl.when(z > 0)
        def _():
            move(rank, s, z_send.at[18 + s], left).wait_send()

    @pl.loop(0, ZL)
    def _(at):
        @pl.when(((at < z) & (z < ZL - 1)) | ((at > z) & (z > 0)))
        def _():
            for s in (0, 1):
                move(rank, s, z_send.at[at * 2 + s], right).wait_send()

    @pl.loop(0, 3 * ZL)
    def _(j):
        move(rank, 0, up_send.at[j], up).wait_send()
        move(rank, 0, down_send.at[j], down).wait_send()

    @pl.loop(0, 2 * Y * ZL)
    def _(j):
        move(rank, 0, mate_send.at[j], mate).wait_send()


def per_device(queries, self_kv, image_kv, cross_gate, lengths):
    vmem = pl.BlockSpec(memory_space=pltpu.VMEM)
    dma = pltpu.SemaphoreType.DMA
    return pl.pallas_call(
        attention_kernel,
        out_shape=jax.ShapeDtypeStruct(queries.shape, queries.dtype),
        in_specs=[
            vmem,
            pl.BlockSpec(memory_space=pl.ANY),
            vmem,
            vmem,
            pl.BlockSpec(memory_space=pltpu.SMEM),
        ],
        out_specs=vmem,
        scratch_shapes=[
            pltpu.VMEM((2, 64 * B, 2 * D), jnp.bfloat16),
            pltpu.VMEM((X, 2, 2, D), jnp.bfloat16),
            pltpu.VMEM((8, ZR, X, 2, D), jnp.bfloat16),
            pltpu.VMEM((2, D, ROWS), jnp.bfloat16),
            pltpu.VMEM((4, D, ROWS), jnp.float32),
            pltpu.VMEM((4, 1, ROWS), jnp.float32),
            pltpu.VMEM((4, 1, ROWS), jnp.float32),
            pltpu.VMEM((2, 1, ROWS), jnp.int32),
            dma((128,)),
            dma((20,)),
            dma((24,)),
            dma((24,)),
            dma((64,)),
            dma((X,)),
            dma((X,)),
            dma((ZR,)),
            dma((ZR,)),
            dma((8,)),
            dma((7,)),
            dma((4,)),
            pltpu.SemaphoreType.REGULAR,
        ],
        compiler_params=pltpu.CompilerParams(
            collective_id=0, has_side_effects=True, vmem_limit_bytes=56 * 1024 * 1024
        ),
    )(queries, self_kv, image_kv.reshape(X, 2, 2, D), cross_gate.reshape(1, 4), lengths)


def solution(mesh):
    placed = (
        P(None, ("ctx", "section"), "tp"),
        P(None, ("ctx", "section"), None),
        P(("ctx", "tp", "section"), None),
        P("tp"),
        P(),
    )
    return jax.shard_map(
        per_device,
        mesh=mesh,
        in_specs=placed,
        out_specs=P(None, ("ctx", "section"), "tp"),
        check_vma=False,
    )
```

```python
import functools
import math

import jax
import jax.numpy as jnp
from jax import lax
from jax.experimental import pallas as pl
from jax.experimental.pallas import tpu as pltpu
from jax.sharding import PartitionSpec as P

HQ = 64
KVH = 8
D = 128
B = 128
ZL = 8
ZR = 32
Y = 4
X = 4
ROWS = 512
CHUNK = 512
EARLY = 20
NEG = -1e30
SCALE = math.log2(math.e) / math.sqrt(D)
MESH = pl.DeviceIdType.MESH


def attention_kernel(
    q_ref, kv_ref, img_ref, gate_ref, len_ref, out_ref,
    kv_all, xrows, img_all, qt, acc, best, total, limits,
    kv_recv, z_send, up_send, down_send, mate_send,
    x_recv, x_send, row_recv, row_send, img_recv, img_send, local, token,
):
    ctx = lax.axis_index("ctx")
    tp = lax.axis_index("tp")
    z = lax.axis_index("section")
    y, c = ctx // 2, ctx % 2
    x, zh = tp // 4, tp % 4
    zp = zh * ZL + z
    head = tp // 2
    rank = ctx * ZL + z

    def z_line(at):
        return {"tp": x * 4 + at // ZL, "section": at % ZL}

    right, left = z_line(jnp.minimum(zp + 1, ZR - 1)), z_line(jnp.maximum(zp - 1, 0))
    up = {"ctx": ((y + 1) % Y) * 2 + c}
    down = {"ctx": ((y + Y - 1) % Y) * 2 + c}
    mate = {"ctx": y * 2 + (1 - c)}

    def x_peer(step):
        return {"tp": ((x + step) % X) * 4 + zh}

    def span(block):
        return pl.ds(pl.multiple_of(block * B, B), B)

    def piece(block, s):
        return kv_all.at[s, span(block), :]

    def remote(src, dst, send_sem, recv_sem, to):
        return pltpu.make_async_remote_copy(
            src_ref=src, dst_ref=dst, send_sem=send_sem, recv_sem=recv_sem,
            device_id=to, device_id_type=MESH,
        )

    def move(block, s, send_sem, to):
        return remote(piece(block, s), piece(block, s), send_sem, kv_recv.at[block * 2 + s], to)

    own_cols = pl.ds(pl.multiple_of(head * 2 * D, 2 * D), 2 * D)
    own_kv = [
        pltpu.make_async_copy(kv_ref.at[s, :, own_cols], piece(rank, s), local.at[s]) for s in (0, 1)
    ]
    for cp in own_kv:
        cp.start()

    barrier = pltpu.get_barrier_semaphore()
    peers = (up, down, mate, x_peer(1), x_peer(2), x_peer(3))
    for peer in peers:
        pl.semaphore_signal(barrier, inc=1, device_id=peer, device_id_type=MESH)

    def greet(at):
        pl.semaphore_signal(barrier, inc=1, device_id=z_line(at), device_id_type=MESH)

    @pl.when(zp > 0)
    def _():
        greet(zp - 1)

    @pl.when((zp >= EARLY - 1) & (zp < ZR - 1))
    def _():
        greet(zp + 1)

    @pl.loop(zp + 1, EARLY)
    def _(at):
        greet(at)

    @pl.when(zp < ZL)
    def _():
        @pl.loop(EARLY, ZR)
        def _(at):
            greet(at)

    lower = jnp.where(zp < EARLY, zp, ZL)
    below_is_extra = jnp.where(zp < EARLY, 0, 1)
    above_is_there = jnp.where(zp < ZR - 1, 1, 0)
    pl.semaphore_wait(barrier, len(peers) + lower + below_is_extra + above_is_there)

    @pl.when(zp == EARLY - 1)
    def _():
        pl.semaphore_signal(token, inc=1, device_id=right, device_id_type=MESH)

    def x_move(to, src, step):
        return remote(img_ref.at[to], xrows.at[:, src], x_send.at[step], x_recv.at[src], x_peer(step))

    def row_move(to, src):
        return remote(
            xrows.at[to // 16], img_all.at[ctx, src], row_send.at[to], row_recv.at[src], z_line(to)
        )

    own_x = pltpu.make_async_copy(img_ref.at[x], xrows.at[:, x], local.at[2])
    own_z = pltpu.make_async_copy(xrows.at[zp // 16], img_all.at[ctx, zp], local.at[3])

    def rows_down():
        for step in (1, 2, 3):
            src = (x + X - step) % X
            x_move(x, src, step).wait_recv()
        own_x.wait()
        own_z.start()

        @pl.loop(0, lower)
        def _(at):
            row_move(at, zp).start()

    def rows_down_late():
        @pl.when(zp >= EARLY)
        def _():
            pl.semaphore_wait(token, 1)

            @pl.when(zp < ZR - 1)
            def _():
                pl.semaphore_signal(token, inc=1, device_id=right, device_id_type=MESH)

            @pl.loop(ZL, zp)
            def _(at):
                row_move(at, zp).start()

    def rows_back(first, last):
        @pl.loop(first, last)
        def _(at):
            row_move(at, at).wait_recv()
            row_move(at, zp).start()

    own_x.start()
    for step in (1, 2, 3):
        x_move((x + step) % X, x, step).start()

    def mate_slot(row, at, s):
        return mate_send.at[(row * ZL + at) * 2 + s]

    def block_of(row, at):
        return (row * 2 + c) * ZL + at

    def spread(at, s):
        block = block_of(y, at)
        move(block, s, up_send.at[at * 2 + s], up).start()
        move(block, s, down_send.at[at * 2 + s], down).start()
        move(block, s, mate_slot(y, at, s), mate).start()

    def z_step(d, s):
        @pl.when(z - d >= 0)
        def _():
            at = z - d
            move(block_of(y, at), s, z_send.at[at * 2 + s], right).wait_recv()

            @pl.when(z < ZL - 1)
            def _():
                move(block_of(y, at), s, z_send.at[at * 2 + s], right).start()

            spread(at, s)

        @pl.when(z + d < ZL)
        def _():
            at = z + d
            move(block_of(y, at), s, z_send.at[at * 2 + s], left).wait_recv()

            @pl.when(z > 0)
            def _():
                move(block_of(y, at), s, z_send.at[at * 2 + s], left).start()

            spread(at, s)

    below, above, across = (y + Y - 1) % Y, (y + 1) % Y, (y + 2) % Y

    def y_item(at, s):
        block = block_of(below, at)
        move(block, s, up_send.at[0], up).wait_recv()
        if s == 0:
            move(block, s, up_send.at[2 * ZL + at], up).start()
        move(block, s, mate_slot(below, at, s), mate).start()
        block = block_of(above, at)
        move(block, s, down_send.at[0], down).wait_recv()
        if s == 1:
            move(block, s, down_send.at[2 * ZL + at], down).start()
        move(block, s, mate_slot(above, at, s), mate).start()

    def across_item(at, s):
        block = block_of(across, at)
        move(block, s, up_send.at[0], up).wait_recv()
        move(block, s, mate_slot(across, at, s), mate).start()

    def both_sides(d, item):
        for s in (0, 1):
            @pl.when(z - d >= 0)
            def _():
                item(z - d, s)

            @pl.when(z + d < ZL)
            def _():
                item(z + d, s)

    for s in (0, 1):
        own_kv[s].wait()

        @pl.when(z < ZL - 1)
        def _():
            move(rank, s, z_send.at[16 + s], right).start()

        @pl.when(z > 0)
        def _():
            move(rank, s, z_send.at[18 + s], left).start()

        spread(z, s)

    for s in (0, 1):
        for h in range(4):
            qt[s, :, h * B : (h + 1) * B] = q_ref[s, :, h * D : (h + 1) * D].T

    key_iota = lax.broadcasted_iota(jnp.int32, (CHUNK, ROWS), 0)
    query_pos = rank * B + lax.broadcasted_iota(jnp.int32, (1, ROWS), 1) % B
    for s in (0, 1):
        limits[s] = jnp.minimum(query_pos + 1, len_ref[s])

    def start_rows():
        best[...] = jnp.full_like(best, NEG)
        total[...] = jnp.zeros_like(total)
        acc[...] = jnp.zeros_like(acc)

    def fold(jobs, at):
        scores = []
        for s, (keys, _, limit) in enumerate(jobs):
            raw = jnp.dot(keys, qt[s], preferred_element_type=jnp.float32) * SCALE
            scores.append(raw if limit is None else jnp.where(key_iota < limit, raw, NEG))
        for s, (_, values, _) in enumerate(jobs):
            old = best[at + s]
            new = jnp.maximum(old, jnp.max(scores[s], axis=0, keepdims=True))
            weights = jnp.exp2(scores[s] - new)
            shrink = jnp.exp2(old - new)
            best[at + s] = new
            total[at + s] = total[at + s] * shrink + jnp.sum(weights, axis=0, keepdims=True)
            acc[at + s] = acc[at + s] * shrink + lax.dot_general(
                values, weights.astype(jnp.bfloat16), (((0,), (0,)), ((), ())),
                preferred_element_type=jnp.float32,
            )

    near = z // 4
    far = 1 - near

    def fold_half(row, core, half):
        block = (row * 2 + core) * ZL + half * 4

        @pl.when(core != c)
        def _():
            @pl.loop(0, 4)
            def _(k):
                for s in (0, 1):
                    move(block + k, s, up_send.at[0], mate).wait_recv()

        @pl.when(block // 4 <= rank // 4)
        def _():
            first = pl.multiple_of(block * B, CHUNK)

            keys = pl.ds(first, CHUNK)
            fold([(kv_all[s, keys, :D], kv_all[s, keys, D:], limits[s] - first) for s in (0, 1)], 0)

    def gather_steps(d):
        z_step(d, 0)
        z_step(d, 1)

    start_rows()
    gather_steps(1)
    rows_down()
    rows_down_late()
    gather_steps(2)
    y_item(z, 0)
    y_item(z, 1)
    gather_steps(3)

    @pl.loop(0, 2)
    def _(t):
        gather_steps(4 + 2 * t)
        fold_half(y, (c + t) % 2, near)
        both_sides(1 + t, y_item)
        gather_steps(5 + 2 * t)

    run_end = (zh + 1) * ZL
    rows_back(zp + 1, run_end)
    both_sides(3, y_item)

    def neighbour_row(t):
        return (y + 3 + 2 * (t // 2)) % Y

    @pl.loop(0, 2)
    def _(t):
        fold_half(y, (c + t) % 2, far)

    @pl.when(zp >= ZL)
    def _():
        rows_back(run_end, ZR)

    @pl.loop(0, 4)
    def _(t):
        both_sides(4 + t, y_item)
        fold_half(neighbour_row(t), (c + t) % 2, near)

        @pl.when((t == 1) & (zp < ZL))
        def _():
            rows_back(run_end, ZR)

    across_item(z, 0)
    across_item(z, 1)

    @pl.loop(0, zp)
    def _(at):
        row_move(zp, at).wait_recv()

    own_z.wait()

    def img_move(at, send_sem, to):
        return remote(img_all.at[at], img_all.at[at], send_sem, img_recv.at[at], to)

    img_sends = [img_move(ctx, img_send.at[0], up), img_move(ctx, img_send.at[1], down), img_move(ctx, img_send.at[2], mate)]
    for cp in img_sends:
        cp.start()

    at_below, at_above, at_across = below * 2 + c, above * 2 + c, across * 2 + c
    img_relays = [
        img_move(at_below, img_send.at[3], up), img_move(at_below, img_send.at[4], mate),
        img_move(at_above, img_send.at[5], mate), img_move(at_across, img_send.at[6], mate),
    ]

    @pl.loop(0, 4)
    def _(t):
        fold_half(neighbour_row(t), (c + t) % 2, far)

        @pl.when(t < 3)
        def _():
            both_sides(1 + t, across_item)

    img_move(at_below, img_send.at[0], up).wait_recv()
    img_relays[0].start()
    img_relays[1].start()
    img_move(at_above, img_send.at[0], up).wait_recv()
    img_relays[2].start()

    @pl.loop(0, 2)
    def _(t):
        both_sides(4 + 2 * t, across_item)
        fold_half(across, (c + t) % 2, near)
        both_sides(5 + 2 * t, across_item)

    img_move(at_across, img_send.at[0], up).wait_recv()
    img_relays[3].start()

    @pl.loop(0, 2)
    def _(t):
        fold_half(across, (c + t) % 2, far)

    @pl.loop(0, Y)
    def _(row):
        img_move(row * 2 + 1 - c, img_send.at[0], mate).wait_recv()

    gates = jnp.tanh(gate_ref[...])
    gate_row = jnp.concatenate(
        [jnp.broadcast_to(gates[:, h : h + 1], (1, B)) for h in range(4)], axis=1
    )

    @pl.loop(0, 2)
    def _(n):
        pairs = img_all[pl.ds(4 * n, 4)]
        keys, values = pairs[:, :, :, 0].reshape(CHUNK, D), pairs[:, :, :, 1].reshape(CHUNK, D)
        fold([(keys, values, None)] * 2, 2)

    for s in (0, 1):
        attended = acc[s] * (1.0 / total[s]) + acc[2 + s] * (gate_row / total[2 + s])
        for h in range(4):
            out_ref[s, :, h * D : (h + 1) * D] = attended[:, h * B : (h + 1) * B].T.astype(jnp.bfloat16)

    for cp in img_sends + img_relays:
        cp.wait_send()
    for step in (1, 2, 3):
        x_move(x, x, step).wait_send()

    @pl.loop(0, ZR)
    def _(to):
        @pl.when(to != zp)
        def _():
            row_move(to, zp).wait_send()

    for s in (0, 1):
        @pl.when(z < ZL - 1)
        def _():
            move(rank, s, z_send.at[16 + s], right).wait_send()

        @pl.when(z > 0)
        def _():
            move(rank, s, z_send.at[18 + s], left).wait_send()

    @pl.loop(0, ZL)
    def _(at):
        @pl.when(((at < z) & (z < ZL - 1)) | ((at > z) & (z > 0)))
        def _():
            for s in (0, 1):
                move(rank, s, z_send.at[at * 2 + s], right).wait_send()

    @pl.loop(0, 3 * ZL)
    def _(j):
        move(rank, 0, up_send.at[j], up).wait_send()
        move(rank, 0, down_send.at[j], down).wait_send()

    @pl.loop(0, 2 * Y * ZL)
    def _(j):
        move(rank, 0, mate_send.at[j], mate).wait_send()


def per_device(queries, self_kv, image_kv, cross_gate, lengths):
    vmem = pl.BlockSpec(memory_space=pltpu.VMEM)
    dma = pltpu.SemaphoreType.DMA
    return pl.pallas_call(
        attention_kernel,
        out_shape=jax.ShapeDtypeStruct(queries.shape, queries.dtype),
        in_specs=[
            vmem,
            pl.BlockSpec(memory_space=pl.ANY),
            vmem,
            vmem,
            pl.BlockSpec(memory_space=pltpu.SMEM),
        ],
        out_specs=vmem,
        scratch_shapes=[
            pltpu.VMEM((2, 64 * B, 2 * D), jnp.bfloat16),
            pltpu.VMEM((2, X, 2, D), jnp.bfloat16),
            pltpu.VMEM((8, ZR, X, 2, D), jnp.bfloat16),
            pltpu.VMEM((2, D, ROWS), jnp.bfloat16),
            pltpu.VMEM((4, D, ROWS), jnp.float32),
            pltpu.VMEM((4, 1, ROWS), jnp.float32),
            pltpu.VMEM((4, 1, ROWS), jnp.float32),
            pltpu.VMEM((2, 1, ROWS), jnp.int32),
            dma((128,)),
            dma((20,)),
            dma((24,)),
            dma((24,)),
            dma((64,)),
            dma((X,)),
            dma((X,)),
            dma((ZR,)),
            dma((ZR,)),
            dma((8,)),
            dma((7,)),
            dma((4,)),
            pltpu.SemaphoreType.REGULAR,
        ],
        compiler_params=pltpu.CompilerParams(
            collective_id=0, has_side_effects=True, vmem_limit_bytes=56 * 1024 * 1024
        ),
    )(queries, self_kv, image_kv.reshape(X, 2, 2, D), cross_gate.reshape(1, 4), lengths)


def solution(mesh):
    placed = (
        P(None, ("ctx", "section"), "tp"),
        P(None, ("ctx", "section"), None),
        P(("ctx", "tp", "section"), None),
        P("tp"),
        P(),
    )
    return jax.shard_map(
        per_device,
        mesh=mesh,
        in_specs=placed,
        out_specs=P(None, ("ctx", "section"), "tp"),
        check_vma=False,
    )
```
